32 devices in a mesh: gx: 8 (over z, y), gy: 4 (over x, core).
Axes of the slice: x: 2, y: 2, z: 4, core: 2. Of those that a mesh axis runs over, the one named last changes fastest.
Arguments:
- cotangent: float32 [2, 128, 1536], P(None, 'gx', 'gy'), may hold values from -12 to 12
- velocity_in: bfloat16 [2, 128, 1536], P(None, 'gx', 'gy'), may hold values from -6 to 6
- hidden_pre1: bfloat16 [64, 128, 1536], P(None, 'gx', 'gy'), may hold values from -6 to 6
- hidden_pre2: bfloat16 [64, 128, 1536], P(None, 'gx', 'gy'), may hold values from -6 to 6
- w_first: bfloat16 [9, 64, 2], replicated, may hold values from -1.5 to 1.5
- w_middle: bfloat16 [9, 64, 64], replicated, may hold values from -0.25 to 0.25
- w_last: bfloat16 [9, 2, 64], replicated, may hold values from -0.25 to 0.25
Outputs:
- grad_velocity: float32 [2, 128, 1536], P(None, 'gx', 'gy')
- grad_first: float32 [9, 64, 2], replicated
- grad_middle: float32 [9, 64, 64], replicated
- grad_last: float32 [9, 2, 64], replicated
- grad_bias1: float32 [64], replicated
- grad_bias2: float32 [64], replicated
The draws below stay inside these ranges and needn't reach their ends.
All inputs are finite; a program needn't handle non-finite values.
Results may differ from the reference program's by a relative error of at most 0.0075.
Values may be sent and summed in bfloat16 or wider, within the bound.
A program may use at most 64 MiB of HBM per device.

```python
import math
import jax
import jax.numpy as jnp
from jax import lax

CH = 64
CX = 16
CY = 384
ITERS = 4
NX = 128
NY = 1536


TWO_PI = 6.283185307179586


def wave_phase(row_wave, col_wave):
    row_index = jnp.arange(NX, dtype=jnp.int32)[:, None]
    col_index = jnp.arange(NY, dtype=jnp.int32)[None, :]
    row_part = (row_wave * row_index % NX).astype(jnp.float32) / NX
    col_part = (col_wave * col_index % NY).astype(jnp.float32) / NY
    return TWO_PI * (row_part + col_part)


def block_levels(key, count, width, lower, upper):
    table = jnp.exp(jax.random.uniform(key, (count // width,), jnp.float32, lower, upper))
    which = jnp.arange(count, dtype=jnp.int32) // width
    return table[which]


def draw_cotangent(key, part):
    keys = jax.random.split(key, 8)
    row_low = max(1, NX // 96)
    row_high = max(row_low, NX // 24) + 1
    col_high = max(1, NY // 24)
    row_waves = jax.random.randint(keys[0], (9,), row_low, row_high)
    col_waves = jax.random.randint(keys[1], (9,), -col_high, col_high + 1)
    phases = jax.random.uniform(keys[2], (9,), jnp.float32, -3.14159, 3.14159)
    amplitudes = jax.random.uniform(keys[3], (8,), jnp.float32, 0.3, 1.2)
    noise = 0.35 * jax.random.truncated_normal(keys[4], -4.0, 4.0, (2, NX, NY), jnp.float32)
    col_noise = block_levels(keys[5], NY, CY, -2.5, 1.5)
    row_noise = block_levels(keys[6], NX, CX, -1.2, 1.2)
    col_smooth = block_levels(keys[7], NY, CY, -1.0, 1.0)
    envelope = jnp.exp(1.15 * jnp.sin(wave_phase(row_waves[8], col_waves[8]) + phases[8]))
    envelope = envelope * row_noise[:, None] * col_noise[None, :]
    components = []
    for comp in range(2):
        smooth = jnp.zeros((NX, NY), jnp.float32)
        for index in range(4):
            which = 4 * comp + index
            smooth = smooth + amplitudes[which] * jnp.sin(wave_phase(row_waves[which], col_waves[which]) + phases[which])
        components.append(smooth * col_smooth[None, :])
    total = jnp.stack(components) + noise * envelope[None, :, :]
    return jnp.clip(total, -12.0, 12.0).astype(jnp.float32)


def level_of(own_key, shape, cuts, least, top_value):
    loudness, own = 1.0, jax.random.fold_in(own_key, 6)
    for axis_at, parts in cuts:
        heights = jnp.exp(jax.random.uniform(jax.random.fold_in(own, axis_at), (parts,), jnp.float32, least / len(cuts), top_value / len(cuts)))
        loudness = loudness * jnp.repeat(heights, shape[axis_at] // parts).reshape([-1 if axis == axis_at else 1 for axis in range(len(shape))])
    return loudness


def bell_draw(key, extent, scale, most, cuts=(), kind=jnp.bfloat16):
    drawn = scale * jax.random.normal(key, extent, jnp.float32)
    if cuts:
        drawn = drawn * level_of(key, extent, cuts, -0.22, 0.18)
    return jnp.clip(drawn, -most, most).astype(kind)


def setup_inputs(seed: int = 0) -> dict:
    arg_keys = jax.random.split(jax.random.key(seed), 8)
    return {
        "cotangent": draw_cotangent(jax.random.fold_in(arg_keys[7], 71), 0),
        "velocity_in": bell_draw(arg_keys[1], (2, NX, NY), 1.0, 6.0, ((1, 8), (2, 4))),
        "hidden_pre1": bell_draw(arg_keys[2], (CH, NX, NY), 1.0, 6.0, ((1, 8), (2, 4))),
        "hidden_pre2": bell_draw(arg_keys[3], (CH, NX, NY), 1.0, 6.0, ((1, 8), (2, 4))),
        "w_first": bell_draw(arg_keys[4], (9, CH, 2), 18 ** -0.5, 1.5),
        "w_middle": bell_draw(arg_keys[5], (9, CH, CH), (9 * CH) ** -0.5, 0.25),
        "w_last": bell_draw(arg_keys[6], (9, 2, CH), (9 * CH) ** -0.5, 0.25),
    }


OFFSETS = ((-1, -1), (-1, 0), (-1, 1), (0, -1), (0, 0), (0, 1), (1, -1), (1, 0), (1, 1))

def moved_to(field, row_step, col_step):
    return jnp.roll(field, (-row_step, -col_step), axis=(1, 2))

def gelu_slope(pre):
    values = pre.astype(jnp.float32)
    _, pullback = jax.vjp(lambda inner: jax.nn.gelu(inner, approximate=True), values)
    return pullback(jnp.ones_like(values))[0]

def apply_stencil(field):
    beside = jnp.roll(field, 2, 0) + jnp.roll(field, -2, 0) + jnp.roll(field, 2, 1)
    beside = beside + jnp.roll(field, -2, 1)
    return field - 0.25 * beside

def conv_back(weights, deltas):
    channels = deltas.shape[0]
    total = jnp.zeros((weights.shape[2], deltas.shape[1] * deltas.shape[2]), jnp.float32)
    for index, (row_step, col_step) in enumerate(OFFSETS):
        shifted = moved_to(deltas, -row_step, -col_step).reshape(channels, -1)
        total = total + lax.dot_general(weights[index], shifted, (((0,), (0,)), ((), ())), preferred_element_type=jnp.float32)
    return total.reshape(weights.shape[2], deltas.shape[1], deltas.shape[2])

def tap_grads(deltas, inputs):
    flat_deltas = deltas.reshape(deltas.shape[0], -1)
    results = []
    for row_step, col_step in OFFSETS:
        shifted = moved_to(inputs, row_step, col_step).reshape(inputs.shape[0], -1)
        results.append(lax.dot_general(flat_deltas, shifted, (((1,), (1,)), ((), ())), preferred_element_type=jnp.float32))
    return jnp.stack(results)

def reference(cotangent, velocity_in, hidden_pre1, hidden_pre2, w_first, w_middle, w_last):
    hidden1 = jax.nn.gelu(hidden_pre1.astype(jnp.float32), approximate=True).astype(jnp.bfloat16)
    hidden2 = jax.nn.gelu(hidden_pre2.astype(jnp.float32), approximate=True).astype(jnp.bfloat16)
    slope1 = gelu_slope(hidden_pre1)
    slope2 = gelu_slope(hidden_pre2)
    along_rows = jnp.roll(cotangent[0], -1, 0) - jnp.roll(cotangent[0], 1, 0)
    along_cols = jnp.roll(cotangent[1], -1, 1) - jnp.roll(cotangent[1], 1, 1)
    rhs = -0.5 * (along_rows + along_cols)
    lam = jnp.zeros_like(rhs)
    residual = rhs
    direction = rhs
    norm_now = jnp.sum(residual * residual)
    for step in range(ITERS):
        image = apply_stencil(direction)
        alpha = norm_now / jnp.sum(direction * image)
        lam = lam + alpha * direction
        if step + 1 < ITERS:
            residual = residual - alpha * image
            norm_next = jnp.sum(residual * residual)
            direction = residual + norm_next / norm_now * direction
            norm_now = norm_next
    adjoint_rows = 0.5 * (jnp.roll(lam, 1, 0) - jnp.roll(lam, -1, 0))
    adjoint_cols = 0.5 * (jnp.roll(lam, 1, 1) - jnp.roll(lam, -1, 1))
    adjoint = cotangent + jnp.stack([adjoint_rows, adjoint_cols])
    adjoint_b = adjoint.astype(jnp.bfloat16)
    delta2 = (conv_back(w_last, adjoint_b) * slope2).astype(jnp.bfloat16)
    delta1 = (conv_back(w_middle, delta2) * slope1).astype(jnp.bfloat16)
    grad_velocity = adjoint + conv_back(w_first, delta1)
    factor = 1.0 / math.sqrt(NX * NY)
    grad_last = factor * tap_grads(adjoint_b, hidden2)
    grad_middle = factor * tap_grads(delta2, hidden1)
    grad_first = factor * tap_grads(delta1, velocity_in)
    grad_bias1 = factor * lax.optimization_barrier(jnp.sum(delta1.astype(jnp.float32), axis=(1, 2)))
    grad_bias2 = factor * lax.optimization_barrier(jnp.sum(delta2.astype(jnp.float32), axis=(1, 2)))
    return (grad_velocity, grad_first, grad_middle, grad_last, grad_bias1, grad_bias2)
```

```python
import functools
import math

import jax
import jax.numpy as jnp
from jax import lax
from jax.experimental import pallas as pl
from jax.experimental.pallas import tpu as pltpu
from jax.sharding import PartitionSpec as P

ITERS = 4
MESH = pl.DeviceIdType.MESH
NEIGHBOURS = tuple((dx, dy) for dx in (-1, 0, 1) for dy in (-1, 0, 1) if (dx, dy) != (0, 0))
NT = (((1,), (1,)), ((), ()))
NN = (((1,), (0,)), ((), ()))
C0 = 0.7978845608028654
C1 = 0.044715


def dot(a, b, dims):
    return lax.dot_general(a, b, dims, preferred_element_type=jnp.float32)


def roll_to(x, shift, axis):
    return pltpu.roll(x, shift % x.shape[axis], axis)


def gelu_value(v):
    return 0.5 * v * (1.0 + jnp.tanh(C0 * (v + C1 * (v * v * v))))


def gelu_slope(v):
    square = v * v
    t = jnp.tanh(C0 * (v + C1 * (square * v)))
    return 0.5 * (1.0 + t) + 0.5 * v * (1.0 - t * t) * (C0 * (1.0 + 3.0 * C1 * square))


def greet(peers):
    barrier = pltpu.get_barrier_semaphore()
    for peer in peers:
        pl.semaphore_signal(barrier, inc=1, device_id=peer, device_id_type=MESH)
    pl.semaphore_wait(barrier, len(peers))


def line_peers(nx, ny):
    gx, gy = lax.axis_index("gx"), lax.axis_index("gy")
    along_x = [(lax.rem(gx + k, nx), gy) for k in range(1, nx)]
    along_y = [(gx, lax.rem(gy + k, ny)) for k in range(1, ny)]
    return gx, gy, along_x, along_y


def merge_border(block, axis):
    n = block.shape[axis] - 256
    right = lax.slice_in_dim(block, n, n + 128, axis=axis)
    left = lax.slice_in_dim(block, n + 128, n + 256, axis=axis)
    lane = lax.broadcasted_iota(jnp.int32, right.shape, axis)
    border = jnp.where(lane < 64, right, left)
    return jnp.concatenate([lax.slice_in_dim(block, 0, n, axis=axis), border], axis=axis)


def exchange_kernel(
    nx, ny, cot, vel, pre1, pre2, adj_out, vel_out, pad1, pad2,
    cot_pad, slots_y, slots_x, send, recv, local, send_y, recv_y, send_x, recv_x,
):
    rows, cols = cot.shape[1], cot.shape[2]
    gx, gy, along_x, along_y = line_peers(nx, ny)

    def at(dx, dy):
        return (lax.rem(gx + dx + nx, nx), lax.rem(gy + dy + ny, ny))

    corners = [at(dx, dy) for dx, dy in NEIGHBOURS if dx and dy]
    greet(along_x + along_y + corners)

    def halves(dx, dy, halo):
        source = {1: slice(rows - halo, rows), 0: slice(0, rows), -1: slice(0, halo)}[dx]
        target = {1: slice(0, halo), 0: slice(halo, halo + rows), -1: slice(halo + rows, rows + 2 * halo)}[dx]
        lanes = {1: slice(cols - 128, cols), 0: slice(0, cols), -1: slice(0, 128)}[dy]
        land = {1: slice(cols + 128, cols + 256), 0: slice(0, cols), -1: slice(cols, cols + 128)}[dy]
        return source, target, lanes, land

    def border(index, which, dx, dy):
        if which < 2:
            src, dst = ((cot, cot_pad), (vel, vel_out))[which]
            s, t, a, b = halves(dx, dy, rows)
            src, dst = src.at[:, s, a], dst.at[:, t, b]
        else:
            src, dst = ((pre1, pad1), (pre2, pad2))[which - 2]
            s, t, a, b = halves(dx, dy, which - 1)
            src, dst = src.at[s, :, a], dst.at[t, :, b]
        return pltpu.make_async_remote_copy(
            src_ref=src, dst_ref=dst, send_sem=send.at[which, index], recv_sem=recv.at[which, index],
            device_id=at(dx, dy), device_id_type=MESH,
        )

    copies = [[border(i, which, dx, dy) for i, (dx, dy) in enumerate(NEIGHBOURS)] for which in range(4)]
    own = [
        pltpu.make_async_copy(pre1, pad1.at[1 : rows + 1, :, 0:cols], local.at[0]),
        pltpu.make_async_copy(pre2, pad2.at[2 : rows + 2, :, 0:cols], local.at[1]),
    ]
    for copy in copies[0]:
        copy.start()
    for copy in own:
        copy.start()
    for which in (1, 2, 3):
        for copy in copies[which]:
            copy.start()
    cot_pad[:, rows : 2 * rows, 0:cols] = cot[...]
    vel_out[:, rows : 2 * rows, 0:cols] = vel[...]
    for copy in copies[0]:
        copy.wait_recv()

    c = merge_border(cot_pad[...], 2)
    c0, c1 = c[0], c[1]
    rhs = -0.5 * ((roll_to(c0, -1, 0) - roll_to(c0, 1, 0)) + (roll_to(c1, -1, 1) - roll_to(c1, 1, 1)))
    fields = [rhs]
    for _ in range(ITERS):
        q = fields[-1]
        beside = roll_to(q, 2, 0) + roll_to(q, -2, 0) + roll_to(q, 2, 1)
        fields.append(-0.25 * (beside + roll_to(q, -2, 1)))
    inner = [f[rows : 2 * rows, 0:cols] for f in fields]
    partial = []
    for k in range(2 * ITERS):
        product = inner[k // 2] * inner[(k + 1) // 2]
        total = product[:, 0:128]
        for at_lane in range(128, cols, 128):
            total = total + product[:, at_lane : at_lane + 128]
        partial.append(jnp.sum(total, axis=0, keepdims=True))
    moments = jnp.concatenate(partial, axis=0)

    def share(slots, me, peers, count, send_s, recv_s, value):
        slots[me] = value
        started = []
        for k, peer in enumerate(peers):
            copy = pltpu.make_async_remote_copy(
                src_ref=slots.at[me], dst_ref=slots.at[me], send_sem=send_s.at[k], recv_sem=recv_s.at[k],
                device_id=peer, device_id_type=MESH,
            )
            copy.start()
            started.append(copy)
        for copy in started:
            copy.wait_recv()
        total = slots[0]
        for k in range(1, count):
            total = total + slots[k]
        for copy in started:
            copy.wait_send()
        return total

    moments = share(slots_y, gy, along_y, ny, send_y, recv_y, moments)
    moments = share(slots_x, gx, along_x, nx, send_x, recv_x, moments)
    moments = jnp.sum(moments, axis=1, keepdims=True)
    n = [moments[k : k + 1, 0:1] for k in range(2 * ITERS)]

    zero, one = jnp.zeros_like(n[0]), jnp.ones_like(n[0])
    lam, residual, direction = [zero] * (ITERS + 1), [one] + [zero] * ITERS, [one] + [zero] * ITERS
    norm_now = n[0]
    for step in range(ITERS):
        product = zero
        for i in range(step + 1):
            for j in range(step + 1):
                product = product + direction[i] * direction[j] * (n[i + j] + n[i + j + 1])
        alpha = norm_now / product
        lam = [x + alpha * p for x, p in zip(lam, direction)]
        if step + 1 < ITERS:
            image = [p + below for p, below in zip(direction, [zero] + direction[:-1])]
            residual = [r - alpha * a for r, a in zip(residual, image)]
            norm_next = zero
            for i in range(step + 2):
                for j in range(step + 2):
                    norm_next = norm_next + residual[i] * residual[j] * n[i + j]
            ratio = norm_next / norm_now
            direction = [r + ratio * p for r, p in zip(residual, direction)]
            norm_now = norm_next
    field = lam[0] * fields[0]
    for k in range(1, ITERS):
        field = field + lam[k] * fields[k]
    adj_out[0] = c0 + 0.5 * (roll_to(field, 1, 0) - roll_to(field, -1, 0))
    adj_out[1] = c1 + 0.5 * (roll_to(field, 1, 1) - roll_to(field, -1, 1))

    for copy in own:
        copy.wait()
    for which in (1, 2, 3):
        for copy in copies[which]:
            copy.wait_recv()
    for group in copies:
        for copy in group:
            copy.wait_send()


def conv_kernel(
    adj, vel, pad1, pad2, w_last, w_middle, w_first, spread_out, grads_out,
    adj_rolled, vel_rolled, stack, taps, deltas1, spread, gm, gl, gf,
):
    rows = spread_out.shape[1]
    cols = spread_out.shape[2]
    ch = w_middle.shape[0]
    v = merge_border(vel[...].astype(jnp.float32), 2)
    for b in (-1, 0, 1):
        for k in range(2):
            adj_rolled[2 * (b + 1) + k] = roll_to(adj[k], b, 1) if b else adj[k]
            vel_rolled[2 * (b + 1) + k] = roll_to(v[k], -b, 1) if b else v[k]
    spread[...] = jnp.zeros_like(spread)
    gm[...] = jnp.zeros_like(gm)
    gl[...] = jnp.zeros_like(gl)
    gf[...] = jnp.zeros_like(gf)
    taps[...] = jnp.zeros_like(taps)

    def gather(which, source, row, sign):
        for t in range(9):
            a, b = t // 3 - 1, t % 3 - 1
            for k in range(2):
                taps[which, 2 * t + k : 2 * t + k + 1, :] = source[2 * (b + 1) + k, pl.ds(row + sign * a, 1), :]

    def first(i, _):
        gather(0, adj_rolled, rows + i - 2, -1)
        shifted = taps[0].astype(jnp.bfloat16)
        pre = merge_border(pad2[i].astype(jnp.float32), 1)
        delta = dot(w_last[...], shifted, NN) * gelu_slope(pre)
        delta = delta.astype(jnp.bfloat16)
        wide = delta.astype(jnp.float32)
        base = pl.multiple_of(i * (3 * ch), 3 * ch)
        stack[pl.ds(base, ch), :] = roll_to(wide, -1, 1).astype(jnp.bfloat16)
        stack[pl.ds(base + ch, ch), :] = delta
        stack[pl.ds(base + 2 * ch, ch), :] = roll_to(wide, 1, 1).astype(jnp.bfloat16)
        return 0

    lax.fori_loop(0, rows + 4, first, 0)

    def second(j, _):
        base = pl.multiple_of(j * (3 * ch), 3 * ch)
        pre = merge_border(pad1[j].astype(jnp.float32), 1)
        delta = dot(w_middle[...], stack[pl.ds(base, 9 * ch), :], NN) * gelu_slope(pre)
        delta = delta.astype(jnp.bfloat16)
        deltas1[j] = delta
        e = dot(w_first[...], delta, NN)
        f = roll_to(e[0:8], -1, 1) + e[8:16] + roll_to(e[16:24], 1, 1)
        f = f[:, 0:cols]
        for a in (-1, 0, 1):
            for k in range(2):
                at = 2 * (a + 1) + k
                spread[k, pl.ds(j + 1 + a, 1), :] += f[at : at + 1, :]
        return 0

    lax.fori_loop(0, rows + 2, second, 0)

    ones_row = lax.broadcasted_iota(jnp.int32, (32, cols), 0) == 18

    def third(r, _):
        base = pl.multiple_of((r + 1) * (3 * ch), 3 * ch)
        hidden1 = gelu_value(pad1[r + 1][:, 0:cols].astype(jnp.float32)).astype(jnp.bfloat16)
        gm[...] += dot(stack[pl.ds(base, 9 * ch), 0:cols], hidden1, NT)
        hidden2 = gelu_value(pad2[r + 2][:, 0:cols].astype(jnp.float32)).astype(jnp.bfloat16)
        gather(0, adj_rolled, rows + r, -1)
        gl[...] += dot(taps[0][:, 0:cols].astype(jnp.bfloat16), hidden2, NT)
        gather(1, vel_rolled, rows + r, 1)
        taken = jnp.where(ones_row, 1.0, taps[1][:, 0:cols]).astype(jnp.bfloat16)
        delta2 = stack[pl.ds(base + 4 * ch, ch), 0:cols]
        both = jnp.concatenate([deltas1[r + 1][:, 0:cols], delta2], axis=0)
        gf[...] += dot(taken, both, NT)
        return 0

    lax.fori_loop(0, rows, third, 0)
    for k in range(2):
        spread_out[k] = adj[k, rows : 2 * rows, 0:cols] + spread[k, 2 : rows + 2, :]
    half = gm.shape[0] // 2
    grads_out[...] = jnp.zeros_like(grads_out)
    grads_out[0:half, 0:64] = gm[0:half]
    grads_out[0:half, 64:128] = gm[half:]
    ones = lax.broadcasted_iota(jnp.int32, (24, ch), 0) == 18
    grads_out[half : half + 24, 0:64] = gf[0:24, 0:ch]
    grads_out[half : half + 24, 64:128] = jnp.where(ones, gf[0:24, ch : 2 * ch], gl[0:24])


def reduce_kernel(nx, ny, factor, grads, out, slots_x, slots_y, send1, recv1, send2, recv2, send3, recv3):
    gx, gy, along_x, along_y = line_peers(nx, ny)
    greet(along_x + along_y)

    def copy(src, dst, send, recv, k, peer):
        made = pltpu.make_async_remote_copy(
            src_ref=src, dst_ref=dst, send_sem=send.at[k], recv_sem=recv.at[k], device_id=peer, device_id_type=MESH
        )
        made.start()
        return made

    first = [
        copy(grads.at[peer[0]], slots_x.at[gx], send1, recv1, k, peer) for k, peer in enumerate(along_x)
    ]
    slots_x[gx] = grads[gx]
    for c in first:
        c.wait_recv()
    total = slots_x[0]
    for k in range(1, nx):
        total = total + slots_x[k]
    slots_y[gy] = total
    second = [copy(slots_y.at[gy], slots_y.at[gy], send2, recv2, k, peer) for k, peer in enumerate(along_y)]
    for c in second:
        c.wait_recv()
    total = slots_y[0]
    for k in range(1, ny):
        total = total + slots_y[k]
    out[gx] = factor * total
    third = [copy(out.at[gx], out.at[gx], send3, recv3, k, peer) for k, peer in enumerate(along_x)]
    for c in third:
        c.wait_recv()
    for c in first + second + third:
        c.wait_send()


def per_device(nx, ny, cotangent, velocity_in, hidden_pre1, hidden_pre2, w_first, w_middle, w_last):
    rows, cols = cotangent.shape[1], cotangent.shape[2]
    ch = hidden_pre1.shape[0]
    f32, bf16 = jnp.float32, jnp.bfloat16
    factor = 1.0 / math.sqrt(rows * nx * cols * ny)
    vmem = pl.BlockSpec(memory_space=pltpu.VMEM)
    anywhere = pl.BlockSpec(memory_space=pl.ANY)
    dma = pltpu.SemaphoreType.DMA
    pre1 = jnp.transpose(hidden_pre1, (1, 0, 2))
    pre2 = jnp.transpose(hidden_pre2, (1, 0, 2))
    adj, vel, pad1, pad2 = pl.pallas_call(
        functools.partial(exchange_kernel, nx, ny),
        out_shape=(
            jax.ShapeDtypeStruct((2, 3 * rows, cols + 128), f32),
            jax.ShapeDtypeStruct((2, 3 * rows, cols + 256), bf16),
            jax.ShapeDtypeStruct((rows + 2, ch, cols + 256), bf16),
            jax.ShapeDtypeStruct((rows + 4, ch, cols + 256), bf16),
        ),
        in_specs=[vmem, vmem, anywhere, anywhere],
        out_specs=(vmem, vmem, anywhere, anywhere),
        scratch_shapes=[
            pltpu.VMEM((2, 3 * rows, cols + 256), f32),
            pltpu.VMEM((ny, 8, 128), f32),
            pltpu.VMEM((nx, 8, 128), f32),
            dma((4, 8)), dma((4, 8)), dma((2,)),
            dma((ny,)), dma((ny,)), dma((nx,)), dma((nx,)),
        ],
        compiler_params=pltpu.CompilerParams(collective_id=0, has_side_effects=True),
    )(cotangent, velocity_in, pre1, pre2)

    w_l = jnp.pad(w_last.reshape(18, ch), ((0, 14), (0, 0))).T
    w_m = w_middle.reshape(3, 3, ch, ch)[::-1].reshape(9 * ch, ch).T
    w_f = w_first.reshape(3, 3, ch, 2).transpose(1, 0, 3, 2).reshape(3, 6, ch)
    w_f = jnp.pad(w_f, ((0, 0), (0, 2), (0, 0))).reshape(24, ch)
    packed = 9 * ch // 2 + 24
    chunk = 8 * -(-packed // (8 * nx))
    grad_velocity, grads = pl.pallas_call(
        conv_kernel,
        out_shape=(
            jax.ShapeDtypeStruct((2, rows, cols), f32),
            jax.ShapeDtypeStruct((nx * chunk, 128), f32),
        ),
        in_specs=[vmem] * 7,
        out_specs=(vmem, vmem),
        scratch_shapes=[
            pltpu.VMEM((6, 3 * rows, cols + 128), f32),
            pltpu.VMEM((6, 3 * rows, cols + 128), f32),
            pltpu.VMEM(((rows + 4) * 3 * ch, cols + 128), bf16),
            pltpu.VMEM((2, 32, cols + 128), f32),
            pltpu.VMEM((rows + 2, ch, cols + 128), bf16),
            pltpu.VMEM((2, rows + 8, cols), f32),
            pltpu.VMEM((9 * ch, ch), f32),
            pltpu.VMEM((32, ch), f32),
            pltpu.VMEM((32, 2 * ch), f32),
        ],
        compiler_params=pltpu.CompilerParams(vmem_limit_bytes=48 * 2**20),
    )(adj, vel, pad1, pad2, w_l, w_m, w_f)

    summed = pl.pallas_call(
        functools.partial(reduce_kernel, nx, ny, factor),
        out_shape=jax.ShapeDtypeStruct((nx, chunk, 128), f32),
        in_specs=[vmem],
        out_specs=vmem,
        scratch_shapes=[
            pltpu.VMEM((nx, chunk, 128), f32),
            pltpu.VMEM((ny, chunk, 128), f32),
            dma((nx,)), dma((nx,)), dma((ny,)), dma((ny,)), dma((nx,)), dma((nx,)),
        ],
        compiler_params=pltpu.CompilerParams(collective_id=1, has_side_effects=True),
    )(grads.reshape(nx, chunk, 128))
    summed = summed.reshape(nx * chunk, 128)
    half = 9 * ch // 2
    middle = jnp.concatenate([summed[:half, :ch], summed[:half, ch:]], axis=0)
    middle = middle.reshape(3, 3, ch, ch)[::-1].reshape(9, ch, ch)
    small = summed[half : half + 24]
    grad_first = small[:18, :ch].reshape(9, 2, ch).transpose(0, 2, 1)
    grad_last = small[:18, ch:].reshape(9, 2, ch)
    return grad_velocity, grad_first, middle, grad_last, small[18, :ch], small[18, ch:]


def solution(mesh):
    whole = P(None, "gx", "gy")
    return jax.shard_map(
        functools.partial(per_device, mesh.shape["gx"], mesh.shape["gy"]),
        mesh=mesh,
        in_specs=(whole, whole, whole, whole, P(), P(), P()),
        out_specs=(whole, P(), P(), P(), P(), P()),
        check_vma=False,
    )
```

```python
import functools
import math

import jax
import jax.numpy as jnp
from jax import lax
from jax.experimental import pallas as pl
from jax.experimental.pallas import tpu as pltpu
from jax.sharding import PartitionSpec as P

ITERS = 4
MESH = pl.DeviceIdType.MESH
NEIGHBOURS = tuple((dx, dy) for dx in (-1, 0, 1) for dy in (-1, 0, 1) if (dx, dy) != (0, 0))
NT = (((1,), (1,)), ((), ()))
NN = (((1,), (0,)), ((), ()))
C0 = 0.7978845608028654
C1 = 0.044715


def dot(a, b, dims):
    return lax.dot_general(a, b, dims, preferred_element_type=jnp.float32)


def roll_to(x, shift, axis):
    return pltpu.roll(x, shift % x.shape[axis], axis)


def gelu_both(v):
    square = v * v
    half = 0.5 * (1.0 + jnp.tanh(v * (C0 + (C0 * C1) * square)))
    value = v * half
    return value, half + (value * (1.0 - half)) * (2.0 * C0 + (6.0 * C0 * C1) * square)


def greet(peers):
    barrier = pltpu.get_barrier_semaphore()
    for peer in peers:
        pl.semaphore_signal(barrier, inc=1, device_id=peer, device_id_type=MESH)
    pl.semaphore_wait(barrier, len(peers))


def line_peers(nx, ny):
    gx, gy = lax.axis_index("gx"), lax.axis_index("gy")
    along_x = [(lax.rem(gx + k, nx), gy) for k in range(1, nx)]
    along_y = [(gx, lax.rem(gy + k, ny)) for k in range(1, ny)]
    return gx, gy, along_x, along_y


def merge_border(block, axis):
    n = block.shape[axis] - 256
    right = lax.slice_in_dim(block, n, n + 128, axis=axis)
    left = lax.slice_in_dim(block, n + 128, n + 256, axis=axis)
    lane = lax.broadcasted_iota(jnp.int32, right.shape, axis)
    border = jnp.where(lane < 64, right, left)
    return jnp.concatenate([lax.slice_in_dim(block, 0, n, axis=axis), border], axis=axis)


def fused_kernel(
    nx, ny, factor, cot, vel, pre1, pre2, edges, w_last, w_middle, w_first,
    spread_out, middle_out, last_out, small_out,
    cot_pad, vel_pad, edge_in, halo1, halo2, slots_y, slots_x, grads, sums_x, sums_y, gathered, few_y, few_x,
    adj, adj_rolled, vel_rolled, slope1, slope2, hidden1, hidden2, stack, taps, spread, gm, gl, gf,
    send, recv, send_y, recv_y, send_x, recv_x,
):
    rows, cols = cot.shape[1], cot.shape[2]
    ch = pre1.shape[1]
    f32, bf16 = jnp.float32, jnp.bfloat16
    gx, gy, along_x, along_y = line_peers(nx, ny)

    def at(dx, dy):
        return (lax.rem(gx + dx + nx, nx), lax.rem(gy + dy + ny, ny))

    corners = [at(dx, dy) for dx, dy in NEIGHBOURS if dx and dy]
    greet(along_x + along_y + corners)

    def remote(src, dst, which, index, peer):
        return pltpu.make_async_remote_copy(
            src_ref=src, dst_ref=dst, send_sem=send.at[which, index], recv_sem=recv.at[which, index],
            device_id=peer, device_id_type=MESH,
        )

    def block_copy(src, dst, which, index, dx, dy):
        t = rows * (1 - dx)
        lanes = {1: slice(cols - 128, cols), 0: slice(0, cols), -1: slice(0, 128)}[dy]
        land = {1: slice(cols + 128, cols + 256), 0: slice(0, cols), -1: slice(cols, cols + 128)}[dy]
        return remote(src.at[:, :, lanes], dst.at[:, t : t + rows, land], which, index, at(dx, dy))

    cot_copies = [block_copy(cot, cot_pad, 0, i, dx, dy) for i, (dx, dy) in enumerate(NEIGHBOURS)]
    vel_copies = [block_copy(vel, vel_pad, 1, i, dx, dy) for i, (dx, dy) in enumerate(NEIGHBOURS)]
    edge_copies = [
        remote(edges.at[(1 + dy) // 2], edge_in.at[(1 + dy) // 2, 1 - dx], 2, i, at(dx, dy))
        for i, (dx, dy) in enumerate(NEIGHBOURS) if dy
    ]
    row_copies = [
        remote(pre2.at[rows - 2 : rows], halo2.at[0:2], 3, 0, at(1, 0)),
        remote(pre2.at[0:2], halo2.at[2:4], 3, 1, at(-1, 0)),
        remote(pre1.at[rows - 1 : rows], halo1.at[0:1], 3, 2, at(1, 0)),
        remote(pre1.at[0:1], halo1.at[1:2], 3, 3, at(-1, 0)),
    ]
    for copy in cot_copies + edge_copies + row_copies + vel_copies:
        copy.start()
    cot_pad[:, rows : 2 * rows, 0:cols] = cot[...]
    vel_pad[:, rows : 2 * rows, 0:cols] = vel[...]
    spread[...] = jnp.zeros_like(spread)
    gm[...] = jnp.zeros_like(gm)
    gl[...] = jnp.zeros_like(gl)
    gf[...] = jnp.zeros_like(gf)
    taps[...] = jnp.zeros_like(taps)

    def activate(r, _):
        value, slope = gelu_both(pre2[r].astype(f32))
        hidden2[r] = value.astype(bf16)
        slope2[r + 2, :, 0:cols] = slope
        value, slope = gelu_both(pre1[r].astype(f32))
        hidden1[r] = value.astype(bf16)
        slope1[r + 1, :, 0:cols] = slope
        return 0

    for copy in cot_copies:
        copy.wait_recv()
    c = merge_border(cot_pad[...], 2)
    c0, c1 = c[0], c[1]
    rhs = -0.5 * ((roll_to(c0, -1, 0) - roll_to(c0, 1, 0)) + (roll_to(c1, -1, 1) - roll_to(c1, 1, 1)))
    fields = [rhs]
    for _ in range(ITERS):
        q = fields[-1]
        beside = roll_to(q, 2, 0) + roll_to(q, -2, 0) + roll_to(q, 2, 1)
        fields.append(-0.25 * (beside + roll_to(q, -2, 1)))
    inner = [f[rows : 2 * rows, 0:cols] for f in fields]
    partial = []
    for k in range(2 * ITERS):
        product = inner[k // 2] * inner[(k + 1) // 2]
        total = product[:, 0:128]
        for at_lane in range(128, cols, 128):
            total = total + product[:, at_lane : at_lane + 128]
        partial.append(jnp.sum(total, axis=0, keepdims=True))
    moments = jnp.concatenate(partial, axis=0)

    def begin(slots, me, peers, sems, which):
        started = []
        for k, peer in enumerate(peers):
            copy = pltpu.make_async_remote_copy(
                src_ref=slots.at[me], dst_ref=slots.at[me], send_sem=sems[0].at[which, k],
                recv_sem=sems[1].at[which, k], device_id=peer, device_id_type=MESH,
            )
            copy.start()
            started.append(copy)
        return started

    def finish(slots, count, started):
        for copy in started:
            copy.wait_recv()
        total = slots[0]
        for k in range(1, count):
            total = total + slots[k]
        for copy in started:
            copy.wait_send()
        return total

    sems_y, sems_x = (send_y, recv_y), (send_x, recv_x)
    slots_y[gy] = moments
    started = begin(slots_y, gy, along_y, sems_y, 0)
    lax.fori_loop(0, rows // 2, activate, 0)
    slots_x[gx] = finish(slots_y, ny, started)
    started = begin(slots_x, gx, along_x, sems_x, 0)
    lax.fori_loop(rows // 2, rows, activate, 0)

    for copy in row_copies + edge_copies:
        copy.wait_recv()
    lane = lax.broadcasted_iota(jnp.int32, (ch, 128), 1)
    place = lax.rem(lane, 64)
    top = place < jnp.where(lane < 64, 4, 2)
    bottom = place >= jnp.where(lane < 64, 36, 34)
    sides = []
    for side in range(2):
        mid = jnp.where(top, pltpu.roll(edge_in[side, 0], 96, 1), edge_in[side, 1])
        sides.append(jnp.where(bottom, pltpu.roll(edge_in[side, 2], 32, 1), mid))

    def edge_slope(offset):
        right = pltpu.roll(sides[0], lax.rem(256 - offset, 128), 1)
        left = pltpu.roll(sides[1], lax.rem(254 - offset, 128), 1)
        return gelu_both(jnp.where(lane < 64, right, left))[1]

    def edge2(i, _):
        slope2[i, :, cols : cols + 128] = edge_slope(2 * i)
        return 0

    def edge1(j, _):
        slope1[j, :, cols : cols + 128] = edge_slope(64 + 2 * j)
        return 0

    lax.fori_loop(0, rows + 4, edge2, 0)
    lax.fori_loop(0, rows + 2, edge1, 0)
    for i, row in enumerate((0, 1, rows + 2, rows + 3)):
        slope2[row, :, 0:cols] = gelu_both(halo2[i].astype(f32))[1]
    for i, row in enumerate((0, rows + 1)):
        slope1[row, :, 0:cols] = gelu_both(halo1[i].astype(f32))[1]
    for copy in vel_copies:
        copy.wait_recv()
    v = merge_border(vel_pad[...].astype(f32), 2)
    for b in (-1, 0, 1):
        for k in range(2):
            vel_rolled[2 * (b + 1) + k] = roll_to(v[k], -b, 1) if b else v[k]

    moments = jnp.sum(finish(slots_x, nx, started), axis=1, keepdims=True)
    n = [moments[k : k + 1, 0:1] for k in range(2 * ITERS)]
    zero, one = jnp.zeros_like(n[0]), jnp.ones_like(n[0])
    lam, residual, direction = [zero] * (ITERS + 1), [one] + [zero] * ITERS, [one] + [zero] * ITERS
    norm_now = n[0]
    for step in range(ITERS):
        product = zero
        for i in range(step + 1):
            for j in range(step + 1):
                product = product + direction[i] * direction[j] * (n[i + j] + n[i + j + 1])
        alpha = norm_now / product
        lam = [x + alpha * p for x, p in zip(lam, direction)]
        if step + 1 < ITERS:
            image = [p + below for p, below in zip(direction, [zero] + direction[:-1])]
            residual = [r - alpha * a for r, a in zip(residual, image)]
            norm_next = zero
            for i in range(step + 2):
                for j in range(step + 2):
                    norm_next = norm_next + residual[i] * residual[j] * n[i + j]
            ratio = norm_next / norm_now
            direction = [r + ratio * p for r, p in zip(residual, direction)]
            norm_now = norm_next
    field = lam[0] * fields[0]
    for k in range(1, ITERS):
        field = field + lam[k] * fields[k]
    adj[0] = c0 + 0.5 * (roll_to(field, 1, 0) - roll_to(field, -1, 0))
    adj[1] = c1 + 0.5 * (roll_to(field, 1, 1) - roll_to(field, -1, 1))
    for b in (-1, 0, 1):
        for k in range(2):
            adj_rolled[2 * (b + 1) + k] = roll_to(adj[k], b, 1) if b else adj[k]

    def gather(which, source, row, sign):
        for t in range(9):
            a, b = t // 3 - 1, t % 3 - 1
            for k in range(2):
                taps[which, 2 * t + k : 2 * t + k + 1, :] = source[2 * (b + 1) + k, pl.ds(row + sign * a, 1), :]

    def first(i, own):
        gather(0, adj_rolled, rows + i - 2, -1)
        shifted = taps[0].astype(bf16)
        delta = (dot(w_last[...], shifted, NN) * slope2[i]).astype(bf16)
        wide = delta.astype(f32)
        base = pl.multiple_of(i * (3 * ch), 3 * ch)
        stack[pl.ds(base, ch), :] = roll_to(wide, -1, 1).astype(bf16)
        stack[pl.ds(base + ch, ch), :] = delta
        stack[pl.ds(base + 2 * ch, ch), :] = roll_to(wide, 1, 1).astype(bf16)
        if own:
            gl[...] += dot(shifted[:, 0:cols], hidden2[i - 2], NT)
        return 0

    for low, high, own in ((0, 2, False), (2, rows + 2, True), (rows + 2, rows + 4, False)):
        lax.fori_loop(low, high, lambda i, _, own=own: first(i, own), 0)

    def middle(r, _):
        base = pl.multiple_of((r + 1) * (3 * ch), 3 * ch)
        gm[...] += dot(stack[pl.ds(base, 9 * ch), 0:cols], hidden1[r], NT)
        return 0

    lax.fori_loop(0, rows, middle, 0)
    half = 9 * ch // 2
    chunk = grads.shape[1]
    total_rows = nx * chunk
    lower = jnp.concatenate([gl[0:24], jnp.zeros((24, ch), f32)], axis=1)
    packed = jnp.concatenate([gm[0:half], gm[half : 2 * half]], axis=1)
    packed = jnp.concatenate([packed, lower, jnp.zeros((total_rows - half - 24, 128), f32)], axis=0)
    for k in range(nx):
        grads[k] = packed[k * chunk : (k + 1) * chunk]
    scatter = [
        pltpu.make_async_remote_copy(
            src_ref=grads.at[peer[0]], dst_ref=sums_x.at[gx], send_sem=send_x.at[1, k], recv_sem=recv_x.at[1, k],
            device_id=peer, device_id_type=MESH,
        )
        for k, peer in enumerate(along_x)
    ]
    for copy in scatter:
        copy.start()
    sums_x[gx] = grads[gx]

    ones_row = lax.broadcasted_iota(jnp.int32, (32, cols), 0) == 18

    def second(j, own):
        base = pl.multiple_of(j * (3 * ch), 3 * ch)
        delta = dot(w_middle[...], stack[pl.ds(base, 9 * ch), :], NN) * slope1[j]
        delta = delta.astype(bf16)
        e = dot(w_first[...], delta, NN)
        f = roll_to(e[0:8], -1, 1) + e[8:16] + roll_to(e[16:24], 1, 1)
        f = f[:, 0:cols]
        for a in (-1, 0, 1):
            for k in range(2):
                row = 2 * (a + 1) + k
                spread[k, pl.ds(j + 1 + a, 1), :] += f[row : row + 1, :]
        if own:
            gather(1, vel_rolled, rows + j - 1, 1)
            taken = jnp.where(ones_row, 1.0, taps[1][:, 0:cols]).astype(bf16)
            delta2 = stack[pl.ds(base + 4 * ch, ch), 0:cols]
            gf[...] += dot(taken, jnp.concatenate([delta[:, 0:cols], delta2], axis=0), NT)
        return 0

    half_way = rows // 2 + 1
    second(0, False)
    lax.fori_loop(1, half_way, lambda j, _: second(j, True), 0)
    sums_y[gy] = finish(sums_x, nx, scatter)
    started = begin(sums_y, gy, along_y, sems_y, 1)
    lax.fori_loop(half_way, rows + 1, lambda j, _: second(j, True), 0)
    few_y[gy] = gf[0:24]
    few = begin(few_y, gy, along_y, sems_y, 2)
    gathered[gx] = factor * finish(sums_y, ny, started)
    spreading = begin(gathered, gx, along_x, sems_x, 2)
    few_x[gx] = finish(few_y, ny, few)
    few = begin(few_x, gx, along_x, sems_x, 3)
    second(rows + 1, False)
    for k in range(2):
        spread_out[k] = adj[k, rows : 2 * rows, 0:cols] + spread[k, 2 : rows + 2, :]
    for copy in cot_copies + edge_copies + row_copies + vel_copies:
        copy.wait_send()
    for copy in spreading:
        copy.wait_recv()
    for copy in spreading:
        copy.wait_send()
    whole = jnp.concatenate([gathered[k] for k in range(nx)], axis=0)
    for place_at in range(9):
        t = 3 * (2 - place_at // 3) + place_at % 3
        start = place_at * ch
        for low in range(0, ch, 32):
            here = start + low
            side = 0 if here < half else 64
            here = here % half
            middle_out[t, low : low + 32, :] = whole[here : here + 32, side : side + ch]
    for t in range(9):
        last_out[t] = whole[half + 2 * t : half + 2 * t + 2, 0:ch]
    small_out[...] = factor * finish(few_x, nx, few)


def per_device(nx, ny, cotangent, velocity_in, hidden_pre1, hidden_pre2, w_first, w_middle, w_last):
    rows, cols = cotangent.shape[1], cotangent.shape[2]
    ch = hidden_pre1.shape[0]
    f32, bf16 = jnp.float32, jnp.bfloat16
    factor = 1.0 / math.sqrt(rows * nx * cols * ny)
    vmem = pl.BlockSpec(memory_space=pltpu.VMEM)
    dma = pltpu.SemaphoreType.DMA
    pre1 = jnp.transpose(hidden_pre1, (1, 0, 2))
    pre2 = jnp.transpose(hidden_pre2, (1, 0, 2))

    def edge(low):
        first = hidden_pre1[:, :, low : low + 2].reshape(ch, 2 * rows).astype(f32)
        second = hidden_pre2[:, :, low : low + 2].reshape(ch, 2 * rows).astype(f32)
        return jnp.pad(second, ((0, 0), (4, 124 - 2 * rows))) + jnp.pad(first, ((0, 0), (66, 62 - 2 * rows)))

    edges = jnp.stack([edge(0), edge(cols - 2)])
    w_l = jnp.pad(w_last.reshape(18, ch), ((0, 14), (0, 0))).T
    w_m = w_middle.reshape(3, 3, ch, ch)[::-1].reshape(9 * ch, ch).T
    w_f = w_first.reshape(3, 3, ch, 2).transpose(1, 0, 3, 2).reshape(3, 6, ch)
    w_f = jnp.pad(w_f, ((0, 0), (0, 2), (0, 0))).reshape(24, ch)
    packed = 9 * ch // 2 + 24
    chunk = 8 * -(-packed // (8 * nx))
    wide = cols + 128
    most = max(8, nx, ny)
    grad_velocity, grad_middle, grad_last, small = pl.pallas_call(
        functools.partial(fused_kernel, nx, ny, factor),
        out_shape=(
            jax.ShapeDtypeStruct((2, rows, cols), f32),
            jax.ShapeDtypeStruct((9, ch, ch), f32),
            jax.ShapeDtypeStruct((9, 2, ch), f32),
            jax.ShapeDtypeStruct((24, 128), f32),
        ),
        in_specs=[vmem] * 8,
        out_specs=(vmem,) * 4,
        scratch_shapes=[
            pltpu.VMEM((2, 3 * rows, cols + 256), f32),
            pltpu.VMEM((2, 3 * rows, cols + 256), bf16),
            pltpu.VMEM((2, 3, ch, 128), f32),
            pltpu.VMEM((2, ch, cols), bf16),
            pltpu.VMEM((4, ch, cols), bf16),
            pltpu.VMEM((ny, 8, 128), f32),
            pltpu.VMEM((nx, 8, 128), f32),
            pltpu.VMEM((nx, chunk, 128), f32),
            pltpu.VMEM((nx, chunk, 128), f32),
            pltpu.VMEM((ny, chunk, 128), f32),
            pltpu.VMEM((nx, chunk, 128), f32),
            pltpu.VMEM((ny, 24, 128), f32),
            pltpu.VMEM((nx, 24, 128), f32),
            pltpu.VMEM((2, 3 * rows, wide), f32),
            pltpu.VMEM((6, 3 * rows, wide), f32),
            pltpu.VMEM((6, 3 * rows, wide), f32),
            pltpu.VMEM((rows + 2, ch, wide), f32),
            pltpu.VMEM((rows + 4, ch, wide), f32),
            pltpu.VMEM((rows, ch, cols), bf16),
            pltpu.VMEM((rows, ch, cols), bf16),
            pltpu.VMEM(((rows + 4) * 3 * ch, wide), bf16),
            pltpu.VMEM((2, 32, wide), f32),
            pltpu.VMEM((2, rows + 8, cols), f32),
            pltpu.VMEM((9 * ch, ch), f32),
            pltpu.VMEM((32, ch), f32),
            pltpu.VMEM((32, 2 * ch), f32),
            dma((4, 8)), dma((4, 8)),
            dma((3, ny)), dma((3, ny)), dma((4, nx)), dma((4, nx)),
        ],
        compiler_params=pltpu.CompilerParams(
            collective_id=0, has_side_effects=True, vmem_limit_bytes=48 * 2**20
        ),
    )(cotangent, velocity_in, pre1, pre2, edges, w_l, w_m, w_f)
    grad_first = small[:18, :ch].reshape(9, 2, ch).transpose(0, 2, 1)
    return grad_velocity, grad_first, grad_middle, grad_last, small[18, :ch], small[18, ch:]


def solution(mesh):
    whole = P(None, "gx", "gy")
    return jax.shard_map(
        functools.partial(per_device, mesh.shape["gx"], mesh.shape["gy"]),
        mesh=mesh,
        in_specs=(whole, whole, whole, whole, P(), P(), P()),
        out_specs=(whole, P(), P(), P(), P(), P()),
        check_vma=False,
    )
```

```python
import functools
import math

import jax
import jax.numpy as jnp
from jax import lax
from jax.experimental import pallas as pl
from jax.experimental.pallas import tpu as pltpu
from jax.sharding import PartitionSpec as P

ITERS = 4
MESH = pl.DeviceIdType.MESH
NEIGHBOURS = tuple((dx, dy) for dx in (-1, 0, 1) for dy in (-1, 0, 1) if (dx, dy) != (0, 0))
NT = (((1,), (1,)), ((), ()))
NN = (((1,), (0,)), ((), ()))
C0 = 0.7978845608028654
C1 = 0.044715


def dot(a, b, dims):
    return lax.dot_general(a, b, dims, preferred_element_type=jnp.float32)


def roll_to(x, shift, axis):
    return pltpu.roll(x, shift % x.shape[axis], axis)


def gelu_both(v):
    square = v * v
    half = 0.5 * (1.0 + jnp.tanh(v * (C0 + (C0 * C1) * square)))
    value = v * half
    return value, half + (value * (1.0 - half)) * (2.0 * C0 + (6.0 * C0 * C1) * square)


def greet(peers):
    barrier = pltpu.get_barrier_semaphore()
    for peer in peers:
        pl.semaphore_signal(barrier, inc=1, device_id=peer, device_id_type=MESH)
    pl.semaphore_wait(barrier, len(peers))


def line_peers(nx, ny):
    gx, gy = lax.axis_index("gx"), lax.axis_index("gy")
    along_x = [(lax.rem(gx + k, nx), gy) for k in range(1, nx)]
    along_y = [(gx, lax.rem(gy + k, ny)) for k in range(1, ny)]
    return gx, gy, along_x, along_y


def merge_border(block, axis):
    n = block.shape[axis] - 256
    right = lax.slice_in_dim(block, n, n + 128, axis=axis)
    left = lax.slice_in_dim(block, n + 128, n + 256, axis=axis)
    lane = lax.broadcasted_iota(jnp.int32, right.shape, axis)
    border = jnp.where(lane < 64, right, left)
    return jnp.concatenate([lax.slice_in_dim(block, 0, n, axis=axis), border], axis=axis)


def fused_kernel(
    nx, ny, factor, cot, vel, pre1, pre2, edges, w_last, w_middle, w_first,
    spread_out, middle_out, last_out, small_out,
    cot_pad, vel_pad, edge_in, halo1, halo2, slots_y, slots_x, grads, sums_x, sums_y, gathered, few_y, few_x,
    adj, adj_rolled, vel_rolled, slope1, slope2, hidden1, hidden2, acc, taps, spread, gm, gl, gf,
    send, recv, send_y, recv_y, send_x, recv_x,
):
    rows, cols = cot.shape[1], cot.shape[2]
    ch = pre1.shape[1]
    f32, bf16 = jnp.float32, jnp.bfloat16
    gx, gy, along_x, along_y = line_peers(nx, ny)

    def at(dx, dy):
        return (lax.rem(gx + dx + nx, nx), lax.rem(gy + dy + ny, ny))

    corners = [at(dx, dy) for dx, dy in NEIGHBOURS if dx and dy]
    greet(along_x + along_y + corners)

    def remote(src, dst, which, index, peer):
        return pltpu.make_async_remote_copy(
            src_ref=src, dst_ref=dst, send_sem=send.at[which, index], recv_sem=recv.at[which, index],
            device_id=peer, device_id_type=MESH,
        )

    def block_copy(src, dst, which, index, dx, dy):
        t = rows * (1 - dx)
        lanes = {1: slice(cols - 128, cols), 0: slice(0, cols), -1: slice(0, 128)}[dy]
        land = {1: slice(cols + 128, cols + 256), 0: slice(0, cols), -1: slice(cols, cols + 128)}[dy]
        return remote(src.at[:, :, lanes], dst.at[:, t : t + rows, land], which, index, at(dx, dy))

    cot_copies = [block_copy(cot, cot_pad, 0, i, dx, dy) for i, (dx, dy) in enumerate(NEIGHBOURS)]
    vel_copies = [block_copy(vel, vel_pad, 1, i, dx, dy) for i, (dx, dy) in enumerate(NEIGHBOURS)]
    edge_copies = [
        remote(edges.at[(1 + dy) // 2], edge_in.at[(1 + dy) // 2, 1 - dx], 2, i, at(dx, dy))
        for i, (dx, dy) in enumerate(NEIGHBOURS) if dy
    ]
    row_copies = [
        remote(pre2.at[rows - 2 : rows], halo2.at[0:2], 3, 0, at(1, 0)),
        remote(pre2.at[0:2], halo2.at[2:4], 3, 1, at(-1, 0)),
        remote(pre1.at[rows - 1 : rows], halo1.at[0:1], 3, 2, at(1, 0)),
        remote(pre1.at[0:1], halo1.at[1:2], 3, 3, at(-1, 0)),
    ]
    for copy in cot_copies + edge_copies + row_copies + vel_copies:
        copy.start()
    cot_pad[:, rows : 2 * rows, 0:cols] = cot[...]
    vel_pad[:, rows : 2 * rows, 0:cols] = vel[...]
    spread[...] = jnp.zeros_like(spread)
    gm[...] = jnp.zeros_like(gm)
    gl[...] = jnp.zeros_like(gl)
    gf[...] = jnp.zeros_like(gf)
    tap = lax.broadcasted_iota(jnp.int32, taps.shape, 1)
    taps[...] = jnp.where(tap == 18, 1.0, 0.0)
    hidden1[0:3] = jnp.zeros((3, ch, cols), bf16)
    hidden1[rows + 3 : rows + 6] = jnp.zeros((3, ch, cols), bf16)
    acc[0:2] = jnp.zeros((2,) + acc.shape[1:], f32)

    def activate(r, _):
        value, slope = gelu_both(pre2[r].astype(f32))
        hidden2[r] = value.astype(bf16)
        slope2[r + 2, :, 0:cols] = slope
        value, slope = gelu_both(pre1[r].astype(f32))
        hidden1[r + 3] = value.astype(bf16)
        slope1[r + 1, :, 0:cols] = slope
        return 0

    for copy in cot_copies:
        copy.wait_recv()
    c = merge_border(cot_pad[...], 2)
    c0, c1 = c[0], c[1]
    rhs = -0.5 * ((roll_to(c0, -1, 0) - roll_to(c0, 1, 0)) + (roll_to(c1, -1, 1) - roll_to(c1, 1, 1)))
    fields = [rhs]
    for _ in range(ITERS):
        q = fields[-1]
        beside = roll_to(q, 2, 0) + roll_to(q, -2, 0) + roll_to(q, 2, 1)
        fields.append(-0.25 * (beside + roll_to(q, -2, 1)))
    inner = [f[rows : 2 * rows, 0:cols] for f in fields]
    partial = []
    for k in range(2 * ITERS):
        product = inner[k // 2] * inner[(k + 1) // 2]
        total = product[:, 0:128]
        for at_lane in range(128, cols, 128):
            total = total + product[:, at_lane : at_lane + 128]
        partial.append(jnp.sum(total, axis=0, keepdims=True))
    moments = jnp.concatenate(partial, axis=0)

    def begin(slots, me, peers, sems, which):
        started = []
        for k, peer in enumerate(peers):
            copy = pltpu.make_async_remote_copy(
                src_ref=slots.at[me], dst_ref=slots.at[me], send_sem=sems[0].at[which, k],
                recv_sem=sems[1].at[which, k], device_id=peer, device_id_type=MESH,
            )
            copy.start()
            started.append(copy)
        return started

    def finish(slots, count, started):
        for copy in started:
            copy.wait_recv()
        total = slots[0]
        for k in range(1, count):
            total = total + slots[k]
        for copy in started:
            copy.wait_send()
        return total

    sems_y, sems_x = (send_y, recv_y), (send_x, recv_x)
    slots_y[gy] = moments
    started = begin(slots_y, gy, along_y, sems_y, 0)
    lax.fori_loop(0, rows // 2, activate, 0)
    slots_x[gx] = finish(slots_y, ny, started)
    started = begin(slots_x, gx, along_x, sems_x, 0)
    lax.fori_loop(rows // 2, rows, activate, 0)

    for copy in row_copies + edge_copies:
        copy.wait_recv()
    lane = lax.broadcasted_iota(jnp.int32, (ch, 128), 1)
    place = lax.rem(lane, 64)
    top = place < jnp.where(lane < 64, 4, 2)
    bottom = place >= jnp.where(lane < 64, 36, 34)
    sides = []
    for side in range(2):
        mid = jnp.where(top, pltpu.roll(edge_in[side, 0], 96, 1), edge_in[side, 1])
        sides.append(jnp.where(bottom, pltpu.roll(edge_in[side, 2], 32, 1), mid))

    def edge_slope(offset):
        right = pltpu.roll(sides[0], lax.rem(256 - offset, 128), 1)
        left = pltpu.roll(sides[1], lax.rem(254 - offset, 128), 1)
        return gelu_both(jnp.where(lane < 64, right, left))[1]

    def edge2(i, _):
        slope2[i, :, cols : cols + 128] = edge_slope(2 * i)
        return 0

    def edge1(j, _):
        slope1[j, :, cols : cols + 128] = edge_slope(64 + 2 * j)
        return 0

    lax.fori_loop(0, rows + 4, edge2, 0)
    lax.fori_loop(0, rows + 2, edge1, 0)
    for i, row in enumerate((0, 1, rows + 2, rows + 3)):
        slope2[row, :, 0:cols] = gelu_both(halo2[i].astype(f32))[1]
    for i, row in enumerate((0, rows + 1)):
        slope1[row, :, 0:cols] = gelu_both(halo1[i].astype(f32))[1]
    for copy in vel_copies:
        copy.wait_recv()
    v = merge_border(vel_pad[...].astype(f32), 2)
    for b in (-1, 0, 1):
        for k in range(2):
            vel_rolled[2 * (b + 1) + k] = roll_to(v[k], -b, 1) if b else v[k]

    moments = jnp.sum(finish(slots_x, nx, started), axis=1, keepdims=True)
    n = [moments[k : k + 1, 0:1] for k in range(2 * ITERS)]
    zero, one = jnp.zeros_like(n[0]), jnp.ones_like(n[0])
    lam, residual, direction = [zero] * (ITERS + 1), [one] + [zero] * ITERS, [one] + [zero] * ITERS
    norm_now = n[0]
    for step in range(ITERS):
        product = zero
        for i in range(step + 1):
            for j in range(step + 1):
                product = product + direction[i] * direction[j] * (n[i + j] + n[i + j + 1])
        alpha = norm_now / product
        lam = [x + alpha * p for x, p in zip(lam, direction)]
        if step + 1 < ITERS:
            image = [p + below for p, below in zip(direction, [zero] + direction[:-1])]
            residual = [r - alpha * a for r, a in zip(residual, image)]
            norm_next = zero
            for i in range(step + 2):
                for j in range(step + 2):
                    norm_next = norm_next + residual[i] * residual[j] * n[i + j]
            ratio = norm_next / norm_now
            direction = [r + ratio * p for r, p in zip(residual, direction)]
            norm_now = norm_next
    field = lam[0] * fields[0]
    for k in range(1, ITERS):
        field = field + lam[k] * fields[k]
    adj[0] = c0 + 0.5 * (roll_to(field, 1, 0) - roll_to(field, -1, 0))
    adj[1] = c1 + 0.5 * (roll_to(field, 1, 1) - roll_to(field, -1, 1))
    for b in (-1, 0, 1):
        for k in range(2):
            adj_rolled[2 * (b + 1) + k] = roll_to(adj[k], b, 1) if b else adj[k]

    def gather(which, source, row, sign):
        for t in range(9):
            a, b = t // 3 - 1, t % 3 - 1
            for k in range(2):
                taps[which, 2 * t + k : 2 * t + k + 1, :] = source[2 * (b + 1) + k, pl.ds(row + sign * a, 1), :]

    def first(i, own):
        pair = (i, i + 1)
        for at_pair, row in enumerate(pair):
            gather(at_pair, adj_rolled, rows + row - 2, -1)
        shifted = [taps[at_pair].astype(bf16) for at_pair in range(2)]
        deltas = [(dot(w_last[...], x, NN) * slope2[row]).astype(bf16) for x, row in zip(shifted, pair)]
        stacks = []
        for delta in deltas:
            wide = delta.astype(f32)
            stacks.append(
                jnp.concatenate(
                    [roll_to(wide, -1, 1).astype(bf16), delta, roll_to(wide, 1, 1).astype(bf16)], axis=0
                )
            )
        products = [dot(w_middle[...], x, NN) for x in stacks]
        rights = [hidden1[pl.ds(row, 3)].reshape(3 * ch, cols) for row in pair]
        gm[...] += dot(stacks[0][:, 0:cols], rights[0], NT) + dot(stacks[1][:, 0:cols], rights[1], NT)
        if own:
            both = [jnp.concatenate([hidden2[row - 2], d[:, 0:cols]], axis=0) for row, d in zip(pair, deltas)]
            gl[...] += dot(shifted[0][:, 0:cols], both[0], NT) + dot(shifted[1][:, 0:cols], both[1], NT)
        y, z = products
        acc[i] += y[0:ch]
        acc[i + 1] += y[ch : 2 * ch] + z[0:ch]
        acc[i + 2] = y[2 * ch : 3 * ch] + z[ch : 2 * ch]
        acc[i + 3] = z[2 * ch : 3 * ch]
        return 0

    first(0, False)
    lax.fori_loop(0, rows // 2, lambda k, _: first(2 * k + 2, True), 0)
    first(rows + 2, False)
    half = 9 * ch // 2
    chunk = grads.shape[1]
    total_rows = nx * chunk
    third = 3 * ch // 2
    packed = jnp.concatenate([gm[0:third, 128:192], gm[third : 2 * third, 128:192]], axis=1)
    packed = jnp.concatenate(
        [gm[:, 0:128], packed, gl[0:24], jnp.zeros((total_rows - half - 24, 128), f32)], axis=0
    )
    for k in range(nx):
        grads[k] = packed[k * chunk : (k + 1) * chunk]
    scatter = [
        pltpu.make_async_remote_copy(
            src_ref=grads.at[peer[0]], dst_ref=sums_x.at[gx], send_sem=send_x.at[1, k], recv_sem=recv_x.at[1, k],
            device_id=peer, device_id_type=MESH,
        )
        for k, peer in enumerate(along_x)
    ]
    for copy in scatter:
        copy.start()
    sums_x[gx] = grads[gx]

    def second(pair, own):
        deltas = [(acc[j + 2] * slope1[j]).astype(bf16) for j in pair]
        products = [dot(w_first[...], x, NN) for x in deltas]
        if own:
            for at_pair, j in enumerate(pair):
                gather(2 + at_pair, vel_rolled, rows + j - 1, 1)
            taken = [taps[2 + at_pair][:, 0:cols].astype(bf16) for at_pair in range(2)]
            gf[...] += dot(taken[0], deltas[0][:, 0:cols], NT) + dot(taken[1], deltas[1][:, 0:cols], NT)
        for j, e in zip(pair, products):
            f = roll_to(e[0:8], -1, 1) + e[8:16] + roll_to(e[16:24], 1, 1)
            f = f[:, 0:cols]
            for a in (-1, 0, 1):
                for k in range(2):
                    row = 2 * (a + 1) + k
                    spread[k, pl.ds(j + 1 + a, 1), :] += f[row : row + 1, :]
        return 0

    quarter = rows // 4
    second((0, rows + 1), False)
    lax.fori_loop(0, quarter, lambda k, _: second((2 * k + 1, 2 * k + 2), True), 0)
    sums_y[gy] = finish(sums_x, nx, scatter)
    started = begin(sums_y, gy, along_y, sems_y, 1)
    lax.fori_loop(quarter, rows // 2, lambda k, _: second((2 * k + 1, 2 * k + 2), True), 0)
    few_y[gy] = jnp.concatenate([gf[0:24], jnp.zeros((24, ch), f32)], axis=1)
    few = begin(few_y, gy, along_y, sems_y, 2)
    gathered[gx] = factor * finish(sums_y, ny, started)
    spreading = begin(gathered, gx, along_x, sems_x, 2)
    few_x[gx] = finish(few_y, ny, few)
    few = begin(few_x, gx, along_x, sems_x, 3)
    for k in range(2):
        spread_out[k] = adj[k, rows : 2 * rows, 0:cols] + spread[k, 2 : rows + 2, :]
    for copy in cot_copies + edge_copies + row_copies + vel_copies:
        copy.wait_send()
    for copy in spreading:
        copy.wait_recv()
    for copy in spreading:
        copy.wait_send()
    whole = jnp.concatenate([gathered[k] for k in range(nx)], axis=0)
    for t in range(9):
        a, start = t // 3, (t % 3) * ch
        for low in range(0, ch, 32):
            here = start + low
            side = a * ch
            if a == 2:
                side = 0 if here < third else 64
                here = 3 * ch + here % third
            middle_out[t, low : low + 32, :] = whole[here : here + 32, side : side + ch]
    for t in range(9):
        last_out[t] = whole[half + 2 * t : half + 2 * t + 2, 0:ch]
    small_out[0] = factor * finish(few_x, nx, few)
    small_out[1] = whole[half : half + 24]


def per_device(nx, ny, cotangent, velocity_in, hidden_pre1, hidden_pre2, w_first, w_middle, w_last):
    rows, cols = cotangent.shape[1], cotangent.shape[2]
    ch = hidden_pre1.shape[0]
    f32, bf16 = jnp.float32, jnp.bfloat16
    factor = 1.0 / math.sqrt(rows * nx * cols * ny)
    vmem = pl.BlockSpec(memory_space=pltpu.VMEM)
    dma = pltpu.SemaphoreType.DMA
    pre1 = jnp.transpose(hidden_pre1, (1, 0, 2))
    pre2 = jnp.transpose(hidden_pre2, (1, 0, 2))

    def edge(low):
        first = hidden_pre1[:, :, low : low + 2].reshape(ch, 2 * rows).astype(f32)
        second = hidden_pre2[:, :, low : low + 2].reshape(ch, 2 * rows).astype(f32)
        return jnp.pad(second, ((0, 0), (4, 124 - 2 * rows))) + jnp.pad(first, ((0, 0), (66, 62 - 2 * rows)))

    edges = jnp.stack([edge(0), edge(cols - 2)])
    w_l = jnp.pad(w_last.reshape(18, ch), ((0, 14), (0, 0))).T
    w_m = w_middle.reshape(3, 3, ch, ch).transpose(0, 3, 1, 2).reshape(3 * ch, 3 * ch)
    w_f = w_first.reshape(3, 3, ch, 2).transpose(1, 0, 3, 2).reshape(3, 6, ch)
    w_f = jnp.pad(w_f, ((0, 0), (0, 2), (0, 0))).reshape(24, ch)
    packed = 9 * ch // 2 + 24
    chunk = 8 * -(-packed // (8 * nx))
    wide = cols + 128
    most = max(8, nx, ny)
    grad_velocity, grad_middle, grad_last, small = pl.pallas_call(
        functools.partial(fused_kernel, nx, ny, factor),
        out_shape=(
            jax.ShapeDtypeStruct((2, rows, cols), f32),
            jax.ShapeDtypeStruct((9, ch, ch), f32),
            jax.ShapeDtypeStruct((9, 2, ch), f32),
            jax.ShapeDtypeStruct((2, 24, 128), f32),
        ),
        in_specs=[vmem] * 8,
        out_specs=(vmem,) * 4,
        scratch_shapes=[
            pltpu.VMEM((2, 3 * rows, cols + 256), f32),
            pltpu.VMEM((2, 3 * rows, cols + 256), bf16),
            pltpu.VMEM((2, 3, ch, 128), f32),
            pltpu.VMEM((2, ch, cols), bf16),
            pltpu.VMEM((4, ch, cols), bf16),
            pltpu.VMEM((ny, 8, 128), f32),
            pltpu.VMEM((nx, 8, 128), f32),
            pltpu.VMEM((nx, chunk, 128), f32),
            pltpu.VMEM((nx, chunk, 128), f32),
            pltpu.VMEM((ny, chunk, 128), f32),
            pltpu.VMEM((nx, chunk, 128), f32),
            pltpu.VMEM((ny, 24, 128), f32),
            pltpu.VMEM((nx, 24, 128), f32),
            pltpu.VMEM((2, 3 * rows, wide), f32),
            pltpu.VMEM((6, 3 * rows, wide), f32),
            pltpu.VMEM((6, 3 * rows, wide), f32),
            pltpu.VMEM((rows + 2, ch, wide), f32),
            pltpu.VMEM((rows + 4, ch, wide), f32),
            pltpu.VMEM((rows + 6, ch, cols), bf16),
            pltpu.VMEM((rows, ch, cols), bf16),
            pltpu.VMEM((rows + 6, ch, wide), f32),
            pltpu.VMEM((4, 32, wide), f32),
            pltpu.VMEM((2, rows + 8, cols), f32),
            pltpu.VMEM((3 * ch, 3 * ch), f32),
            pltpu.VMEM((32, 2 * ch), f32),
            pltpu.VMEM((32, ch), f32),
            dma((4, 8)), dma((4, 8)),
            dma((3, ny)), dma((3, ny)), dma((4, nx)), dma((4, nx)),
        ],
        compiler_params=pltpu.CompilerParams(
            collective_id=0, has_side_effects=True, vmem_limit_bytes=48 * 2**20
        ),
    )(cotangent, velocity_in, pre1, pre2, edges, w_l, w_m, w_f)
    grad_first = small[0, :18, :ch].reshape(9, 2, ch).transpose(0, 2, 1)
    return grad_velocity, grad_first, grad_middle, grad_last, small[0, 18, :ch], small[1, 18, ch:]


def solution(mesh):
    whole = P(None, "gx", "gy")
    return jax.shard_map(
        functools.partial(per_device, mesh.shape["gx"], mesh.shape["gy"]),
        mesh=mesh,
        in_specs=(whole, whole, whole, whole, P(), P(), P()),
        out_specs=(whole, P(), P(), P(), P(), P()),
        check_vma=False,
    )
```

```python
import functools
import math

import jax
import jax.numpy as jnp
from jax import lax
from jax.experimental import pallas as pl
from jax.experimental.pallas import tpu as pltpu
from jax.sharding import PartitionSpec as P

ITERS = 4
MESH = pl.DeviceIdType.MESH
NEIGHBOURS = tuple((dx, dy) for dx in (-1, 0, 1) for dy in (-1, 0, 1) if (dx, dy) != (0, 0))
NT = (((1,), (1,)), ((), ()))
NN = (((1,), (0,)), ((), ()))
C0 = 0.7978845608028654
C1 = 0.044715


def dot(a, b, dims):
    return lax.dot_general(a, b, dims, preferred_element_type=jnp.float32)


def roll_to(x, shift, axis):
    return pltpu.roll(x, shift % x.shape[axis], axis)


def gelu_both(v):
    square = v * v
    half = 0.5 * (1.0 + jnp.tanh(v * (C0 + (C0 * C1) * square)))
    value = v * half
    return value, half + (value * (1.0 - half)) * (2.0 * C0 + (6.0 * C0 * C1) * square)


def greet(peers):
    barrier = pltpu.get_barrier_semaphore()
    for peer in peers:
        pl.semaphore_signal(barrier, inc=1, device_id=peer, device_id_type=MESH)
    pl.semaphore_wait(barrier, len(peers))


def line_peers(nx, ny):
    gx, gy = lax.axis_index("gx"), lax.axis_index("gy")
    along_x = [(lax.rem(gx + k, nx), gy) for k in range(1, nx)]
    along_y = [(gx, lax.rem(gy + k, ny)) for k in range(1, ny)]
    return gx, gy, along_x, along_y


def merge_border(block, axis):
    n = block.shape[axis] - 256
    right = lax.slice_in_dim(block, n, n + 128, axis=axis)
    left = lax.slice_in_dim(block, n + 128, n + 256, axis=axis)
    lane = lax.broadcasted_iota(jnp.int32, right.shape, axis)
    border = jnp.where(lane < 64, right, left)
    return jnp.concatenate([lax.slice_in_dim(block, 0, n, axis=axis), border], axis=axis)


def fused_kernel(
    nx, ny, factor, cot, vel, pre1, pre2, w_last, w_taps, w_first,
    spread_out, middle_out, last_out, small_out,
    cot_pad, vel_pad, edge_in, halo1, halo2, slots_y, slots_x, grads, sums_x, sums_y, gathered, few_y, few_x,
    adj, adj_rolled, vel_rolled, slope1, slope2, hidden1, hidden2, acc, edges, w_middle, taps, spread, gm, gl, gf,
    send, recv, send_y, recv_y, send_x, recv_x,
):
    rows, cols = cot.shape[1], cot.shape[2]
    ch = pre1.shape[1]
    f32, bf16 = jnp.float32, jnp.bfloat16
    gx, gy, along_x, along_y = line_peers(nx, ny)

    def at(dx, dy):
        return (lax.rem(gx + dx + nx, nx), lax.rem(gy + dy + ny, ny))

    corners = [at(dx, dy) for dx, dy in NEIGHBOURS if dx and dy]
    greet(along_x + along_y + corners)

    def remote(src, dst, which, index, peer):
        return pltpu.make_async_remote_copy(
            src_ref=src, dst_ref=dst, send_sem=send.at[which, index], recv_sem=recv.at[which, index],
            device_id=peer, device_id_type=MESH,
        )

    def block_copy(src, dst, which, index, dx, dy):
        t = rows * (1 - dx)
        lanes = {1: slice(cols - 128, cols), 0: slice(0, cols), -1: slice(0, 128)}[dy]
        land = {1: slice(cols + 128, cols + 256), 0: slice(0, cols), -1: slice(cols, cols + 128)}[dy]
        return remote(src.at[:, :, lanes], dst.at[:, t : t + rows, land], which, index, at(dx, dy))

    cot_copies = [block_copy(cot, cot_pad, 0, i, dx, dy) for i, (dx, dy) in enumerate(NEIGHBOURS)]
    vel_copies = [block_copy(vel, vel_pad, 1, i, dx, dy) for i, (dx, dy) in enumerate(NEIGHBOURS)]
    edge_copies = [
        remote(edges.at[(1 + dy) // 2], edge_in.at[(1 + dy) // 2, 1 - dx], 2, i, at(dx, dy))
        for i, (dx, dy) in enumerate(NEIGHBOURS) if dy
    ]
    row_copies = [
        remote(pre2.at[rows - 2 : rows], halo2.at[0:2], 3, 0, at(1, 0)),
        remote(pre2.at[0:2], halo2.at[2:4], 3, 1, at(-1, 0)),
        remote(pre1.at[rows - 1 : rows], halo1.at[0:1], 3, 2, at(1, 0)),
        remote(pre1.at[0:1], halo1.at[1:2], 3, 3, at(-1, 0)),
    ]
    for copy in cot_copies + row_copies:
        copy.start()
    lane = lax.broadcasted_iota(jnp.int32, (ch, 128), 1)
    for side in range(2):
        low = (cols - 128) * side
        built = jnp.zeros((ch, 128), f32)
        for r in range(rows):
            for source, to_lane in ((pre2, 2 * r + 4), (pre1, 2 * r + 66)):
                moved = roll_to(source[r, :, low : low + 128].astype(f32), to_lane - 126 * side, 1)
                built = jnp.where((lane == to_lane) | (lane == to_lane + 1), moved, built)
        edges[side] = built.astype(bf16)
    for copy in edge_copies + vel_copies:
        copy.start()
    turned = [w_taps[3 * a : 3 * a + 3].astype(f32).reshape(3 * ch, ch) for a in range(3)]
    for a in range(3):
        w_middle[a * ch : (a + 1) * ch, :] = turned[a].T.astype(bf16)
    cot_pad[:, rows : 2 * rows, 0:cols] = cot[...]
    vel_pad[:, rows : 2 * rows, 0:cols] = vel[...]
    spread[...] = jnp.zeros_like(spread)
    gm[...] = jnp.zeros_like(gm)
    gl[...] = jnp.zeros_like(gl)
    gf[...] = jnp.zeros_like(gf)
    tap = lax.broadcasted_iota(jnp.int32, taps.shape, 1)
    taps[...] = jnp.where(tap == 18, 1.0, 0.0)
    hidden1[0:3] = jnp.zeros((3, ch, cols), bf16)
    hidden1[rows + 3 : rows + 6] = jnp.zeros((3, ch, cols), bf16)
    acc[0:2] = jnp.zeros((2,) + acc.shape[1:], f32)

    def activate(r, _):
        value, slope = gelu_both(pre2[r].astype(f32))
        hidden2[r] = value.astype(bf16)
        slope2[r + 2, :, 0:cols] = slope
        value, slope = gelu_both(pre1[r].astype(f32))
        hidden1[r + 3] = value.astype(bf16)
        slope1[r + 1, :, 0:cols] = slope
        return 0

    for copy in cot_copies:
        copy.wait_recv()
    c = merge_border(cot_pad[...], 2)
    c0, c1 = c[0], c[1]
    rhs = -0.5 * ((roll_to(c0, -1, 0) - roll_to(c0, 1, 0)) + (roll_to(c1, -1, 1) - roll_to(c1, 1, 1)))
    fields = [rhs]
    for _ in range(ITERS):
        q = fields[-1]
        beside = roll_to(q, 2, 0) + roll_to(q, -2, 0) + roll_to(q, 2, 1)
        fields.append(-0.25 * (beside + roll_to(q, -2, 1)))
    inner = [f[rows : 2 * rows, 0:cols] for f in fields]
    partial = []
    for k in range(2 * ITERS):
        product = inner[k // 2] * inner[(k + 1) // 2]
        total = product[:, 0:128]
        for at_lane in range(128, cols, 128):
            total = total + product[:, at_lane : at_lane + 128]
        partial.append(jnp.sum(total, axis=0, keepdims=True))
    moments = jnp.concatenate(partial, axis=0)

    def begin(slots, me, peers, sems, which):
        started = []
        for k, peer in enumerate(peers):
            copy = pltpu.make_async_remote_copy(
                src_ref=slots.at[me], dst_ref=slots.at[me], send_sem=sems[0].at[which, k],
                recv_sem=sems[1].at[which, k], device_id=peer, device_id_type=MESH,
            )
            copy.start()
            started.append(copy)
        return started

    def finish(slots, count, started):
        for copy in started:
            copy.wait_recv()
        total = slots[0]
        for k in range(1, count):
            total = total + slots[k]
        for copy in started:
            copy.wait_send()
        return total

    sems_y, sems_x = (send_y, recv_y), (send_x, recv_x)
    slots_y[gy] = moments
    started = begin(slots_y, gy, along_y, sems_y, 0)
    lax.fori_loop(0, rows // 2, activate, 0)
    slots_x[gx] = finish(slots_y, ny, started)
    started = begin(slots_x, gx, along_x, sems_x, 0)
    lax.fori_loop(rows // 2, rows, activate, 0)

    for copy in row_copies + edge_copies:
        copy.wait_recv()
    place = lax.rem(lane, 64)
    top = place < jnp.where(lane < 64, 4, 2)
    bottom = place >= jnp.where(lane < 64, 36, 34)
    sides = []
    for side in range(2):
        above, beside, below = (edge_in[side, k].astype(f32) for k in range(3))
        mid = jnp.where(top, pltpu.roll(above, 96, 1), beside)
        sides.append(jnp.where(bottom, pltpu.roll(below, 32, 1), mid))

    def edge_slope(offset):
        right = pltpu.roll(sides[0], lax.rem(256 - offset, 128), 1)
        left = pltpu.roll(sides[1], lax.rem(254 - offset, 128), 1)
        return gelu_both(jnp.where(lane < 64, right, left))[1]

    def edge2(i, _):
        slope2[i, :, cols : cols + 128] = edge_slope(2 * i)
        return 0

    def edge1(j, _):
        slope1[j, :, cols : cols + 128] = edge_slope(64 + 2 * j)
        return 0

    lax.fori_loop(0, rows + 4, edge2, 0)
    lax.fori_loop(0, rows + 2, edge1, 0)
    for i, row in enumerate((0, 1, rows + 2, rows + 3)):
        slope2[row, :, 0:cols] = gelu_both(halo2[i].astype(f32))[1]
    for i, row in enumerate((0, rows + 1)):
        slope1[row, :, 0:cols] = gelu_both(halo1[i].astype(f32))[1]
    for copy in vel_copies:
        copy.wait_recv()
    v = merge_border(vel_pad[...].astype(f32), 2)
    for b in (-1, 0, 1):
        for k in range(2):
            vel_rolled[2 * (b + 1) + k] = roll_to(v[k], -b, 1) if b else v[k]

    moments = jnp.sum(finish(slots_x, nx, started), axis=1, keepdims=True)
    n = [moments[k : k + 1, 0:1] for k in range(2 * ITERS)]
    zero, one = jnp.zeros_like(n[0]), jnp.ones_like(n[0])
    lam, residual, direction = [zero] * (ITERS + 1), [one] + [zero] * ITERS, [one] + [zero] * ITERS
    norm_now = n[0]
    for step in range(ITERS):
        product = zero
        for i in range(step + 1):
            for j in range(step + 1):
                product = product + direction[i] * direction[j] * (n[i + j] + n[i + j + 1])
        alpha = norm_now / product
        lam = [x + alpha * p for x, p in zip(lam, direction)]
        if step + 1 < ITERS:
            image = [p + below for p, below in zip(direction, [zero] + direction[:-1])]
            residual = [r - alpha * a for r, a in zip(residual, image)]
            norm_next = zero
            for i in range(step + 2):
                for j in range(step + 2):
                    norm_next = norm_next + residual[i] * residual[j] * n[i + j]
            ratio = norm_next / norm_now
            direction = [r + ratio * p for r, p in zip(residual, direction)]
            norm_now = norm_next
    field = lam[0] * fields[0]
    for k in range(1, ITERS):
        field = field + lam[k] * fields[k]
    adj[0] = c0 + 0.5 * (roll_to(field, 1, 0) - roll_to(field, -1, 0))
    adj[1] = c1 + 0.5 * (roll_to(field, 1, 1) - roll_to(field, -1, 1))
    for b in (-1, 0, 1):
        for k in range(2):
            adj_rolled[2 * (b + 1) + k] = roll_to(adj[k], b, 1) if b else adj[k]

    def gather(which, source, row, sign):
        for t in range(9):
            a, b = t // 3 - 1, t % 3 - 1
            for k in range(2):
                taps[which, 2 * t + k : 2 * t + k + 1, :] = source[2 * (b + 1) + k, pl.ds(row + sign * a, 1), :]

    def first(i, own):
        pair = (i, i + 1)
        for at_pair, row in enumerate(pair):
            gather(at_pair, adj_rolled, rows + row - 2, -1)
        shifted = [taps[at_pair].astype(bf16) for at_pair in range(2)]
        deltas = [(dot(w_last[...], x, NN) * slope2[row]).astype(bf16) for x, row in zip(shifted, pair)]
        stacks = []
        for delta in deltas:
            wide = delta.astype(f32)
            stacks.append(
                jnp.concatenate(
                    [roll_to(wide, -1, 1).astype(bf16), delta, roll_to(wide, 1, 1).astype(bf16)], axis=0
                )
            )
        products = [dot(w_middle[...], x, NN) for x in stacks]
        rights = [hidden1[pl.ds(row, 3)].reshape(3 * ch, cols) for row in pair]
        gm[...] += dot(stacks[0][:, 0:cols], rights[0], NT) + dot(stacks[1][:, 0:cols], rights[1], NT)
        if own:
            both = [jnp.concatenate([hidden2[row - 2], d[:, 0:cols]], axis=0) for row, d in zip(pair, deltas)]
            gl[...] += dot(shifted[0][:, 0:cols], both[0], NT) + dot(shifted[1][:, 0:cols], both[1], NT)
        y, z = products
        acc[i] += y[0:ch]
        acc[i + 1] += y[ch : 2 * ch] + z[0:ch]
        acc[i + 2] = y[2 * ch : 3 * ch] + z[ch : 2 * ch]
        acc[i + 3] = z[2 * ch : 3 * ch]
        return 0

    first(0, False)
    lax.fori_loop(0, rows // 2, lambda k, _: first(2 * k + 2, True), 0)
    first(rows + 2, False)
    half = 9 * ch // 2
    chunk = grads.shape[1]
    total_rows = nx * chunk
    third = 3 * ch // 2
    packed = jnp.concatenate([gm[0:third, 128:192], gm[third : 2 * third, 128:192]], axis=1)
    packed = jnp.concatenate(
        [gm[:, 0:128], packed, gl[0:24], jnp.zeros((total_rows - half - 24, 128), f32)], axis=0
    )
    for k in range(nx):
        grads[k] = packed[k * chunk : (k + 1) * chunk]
    scatter = [
        pltpu.make_async_remote_copy(
            src_ref=grads.at[peer[0]], dst_ref=sums_x.at[gx], send_sem=send_x.at[1, k], recv_sem=recv_x.at[1, k],
            device_id=peer, device_id_type=MESH,
        )
        for k, peer in enumerate(along_x)
    ]
    for copy in scatter:
        copy.start()
    sums_x[gx] = grads[gx]

    def second(pair, own):
        deltas = [(acc[j + 2] * slope1[j]).astype(bf16) for j in pair]
        products = [dot(w_first[...], x, NN) for x in deltas]
        if own:
            for at_pair, j in enumerate(pair):
                gather(2 + at_pair, vel_rolled, rows + j - 1, 1)
            taken = [taps[2 + at_pair][:, 0:cols].astype(bf16) for at_pair in range(2)]
            gf[...] += dot(taken[0], deltas[0][:, 0:cols], NT) + dot(taken[1], deltas[1][:, 0:cols], NT)
        for j, e in zip(pair, products):
            f = roll_to(e[0:8], -1, 1) + e[8:16] + roll_to(e[16:24], 1, 1)
            f = f[:, 0:cols]
            for a in (-1, 0, 1):
                for k in range(2):
                    row = 2 * (a + 1) + k
                    spread[k, pl.ds(j + 1 + a, 1), :] += f[row : row + 1, :]
        return 0

    quarter = rows // 4
    second((0, rows + 1), False)
    lax.fori_loop(0, quarter, lambda k, _: second((2 * k + 1, 2 * k + 2), True), 0)
    sums_y[gy] = finish(sums_x, nx, scatter)
    started = begin(sums_y, gy, along_y, sems_y, 1)
    lax.fori_loop(quarter, rows // 2, lambda k, _: second((2 * k + 1, 2 * k + 2), True), 0)
    few_y[gy] = jnp.concatenate([gf[0:24], jnp.zeros((24, ch), f32)], axis=1)
    few = begin(few_y, gy, along_y, sems_y, 2)
    gathered[gx] = factor * finish(sums_y, ny, started)
    spreading = begin(gathered, gx, along_x, sems_x, 2)
    few_x[gx] = finish(few_y, ny, few)
    few = begin(few_x, gx, along_x, sems_x, 3)
    for k in range(2):
        spread_out[k] = adj[k, rows : 2 * rows, 0:cols] + spread[k, 2 : rows + 2, :]
    for copy in cot_copies + edge_copies + row_copies + vel_copies:
        copy.wait_send()
    for copy in spreading:
        copy.wait_recv()
    for copy in spreading:
        copy.wait_send()
    whole = jnp.concatenate([gathered[k] for k in range(nx)], axis=0)
    for t in range(9):
        a, start = t // 3, (t % 3) * ch
        for low in range(0, ch, 32):
            here = start + low
            side = a * ch
            if a == 2:
                side = 0 if here < third else 64
                here = 3 * ch + here % third
            middle_out[t, low : low + 32, :] = whole[here : here + 32, side : side + ch]
    for t in range(9):
        last_out[t] = whole[half + 2 * t : half + 2 * t + 2, 0:ch]
    small_out[0] = factor * finish(few_x, nx, few)
    small_out[1] = whole[half : half + 24]


def per_device(nx, ny, cotangent, velocity_in, hidden_pre1, hidden_pre2, w_first, w_middle, w_last):
    rows, cols = cotangent.shape[1], cotangent.shape[2]
    ch = hidden_pre1.shape[0]
    f32, bf16 = jnp.float32, jnp.bfloat16
    factor = 1.0 / math.sqrt(rows * nx * cols * ny)
    vmem = pl.BlockSpec(memory_space=pltpu.VMEM)
    dma = pltpu.SemaphoreType.DMA
    pre1 = jnp.transpose(hidden_pre1, (1, 0, 2))
    pre2 = jnp.transpose(hidden_pre2, (1, 0, 2))

    w_l = jnp.pad(w_last.reshape(18, ch), ((0, 14), (0, 0))).T
    w_f = w_first.reshape(3, 3, ch, 2).transpose(1, 0, 3, 2).reshape(3, 6, ch)
    w_f = jnp.pad(w_f, ((0, 0), (0, 2), (0, 0))).reshape(24, ch)
    packed = 9 * ch // 2 + 24
    chunk = 8 * -(-packed // (8 * nx))
    wide = cols + 128
    most = max(8, nx, ny)
    grad_velocity, grad_middle, grad_last, small = pl.pallas_call(
        functools.partial(fused_kernel, nx, ny, factor),
        out_shape=(
            jax.ShapeDtypeStruct((2, rows, cols), f32),
            jax.ShapeDtypeStruct((9, ch, ch), f32),
            jax.ShapeDtypeStruct((9, 2, ch), f32),
            jax.ShapeDtypeStruct((2, 24, 128), f32),
        ),
        in_specs=[vmem] * 7,
        out_specs=(vmem,) * 4,
        scratch_shapes=[
            pltpu.VMEM((2, 3 * rows, cols + 256), f32),
            pltpu.VMEM((2, 3 * rows, cols + 256), bf16),
            pltpu.VMEM((2, 3, ch, 128), bf16),
            pltpu.VMEM((2, ch, cols), bf16),
            pltpu.VMEM((4, ch, cols), bf16),
            pltpu.VMEM((ny, 8, 128), f32),
            pltpu.VMEM((nx, 8, 128), f32),
            pltpu.VMEM((nx, chunk, 128), f32),
            pltpu.VMEM((nx, chunk, 128), f32),
            pltpu.VMEM((ny, chunk, 128), f32),
            pltpu.VMEM((nx, chunk, 128), f32),
            pltpu.VMEM((ny, 24, 128), f32),
            pltpu.VMEM((nx, 24, 128), f32),
            pltpu.VMEM((2, 3 * rows, wide), f32),
            pltpu.VMEM((6, 3 * rows, wide), f32),
            pltpu.VMEM((6, 3 * rows, wide), f32),
            pltpu.VMEM((rows + 2, ch, wide), f32),
            pltpu.VMEM((rows + 4, ch, wide), f32),
            pltpu.VMEM((rows + 6, ch, cols), bf16),
            pltpu.VMEM((rows, ch, cols), bf16),
            pltpu.VMEM((rows + 6, ch, wide), f32),
            pltpu.VMEM((2, ch, 128), bf16),
            pltpu.VMEM((3 * ch, 3 * ch), bf16),
            pltpu.VMEM((4, 32, wide), f32),
            pltpu.VMEM((2, rows + 8, cols), f32),
            pltpu.VMEM((3 * ch, 3 * ch), f32),
            pltpu.VMEM((32, 2 * ch), f32),
            pltpu.VMEM((32, ch), f32),
            dma((4, 8)), dma((4, 8)),
            dma((3, ny)), dma((3, ny)), dma((4, nx)), dma((4, nx)),
        ],
        compiler_params=pltpu.CompilerParams(
            collective_id=0, has_side_effects=True, vmem_limit_bytes=48 * 2**20
        ),
    )(cotangent, velocity_in, pre1, pre2, w_l, w_middle, w_f)
    grad_first = small[0, :18, :ch].reshape(9, 2, ch).transpose(0, 2, 1)
    return grad_velocity, grad_first, grad_middle, grad_last, small[0, 18, :ch], small[1, 18, ch:]


def solution(mesh):
    whole = P(None, "gx", "gy")
    return jax.shard_map(
        functools.partial(per_device, mesh.shape["gx"], mesh.shape["gy"]),
        mesh=mesh,
        in_specs=(whole, whole, whole, whole, P(), P(), P()),
        out_specs=(whole, P(), P(), P(), P(), P()),
        check_vma=False,
    )
```
